32 devices in a mesh: rcv: 16 (over z, x, core), frq: 2 (over y).
Axes of the slice: x: 2, y: 2, z: 4, core: 2. Of those that a mesh axis runs over, the one named last changes fastest.
Arguments:
- spectra: bfloat16 [2, 256, 128, 4096], P(None, None, 'frq', 'rcv'), may hold values from -6 to 6
- virtual_sources: int32 [128], replicated, may hold values from 0 to 4095, as said below
- references: int32 [256], replicated, may hold values from 0 to 4095, as said below
- coda_start: int32 [128], replicated, may hold values from 64 to 255
- coda_end: int32 [128], replicated, may hold values from 384 to 511
Outputs:
- correlations: float32 [2, 128, 256, 4096], P(None, 'frq', None, 'rcv')
The draws below stay inside these ranges and needn't reach their ends.
Inputs may be any that keep to these rules, and one draw needn't show every extreme that they name: `virtual_sources`: distinct receivers; virtual source v is one of the receivers (v // 8) * 256 to (v // 8 + 1) * 256 - 1. `references`: distinct receivers; reference p is one of the receivers (p // 16) * 256 to (p // 16 + 1) * 256 - 1.
All inputs are finite; a program needn't handle non-finite values.
Results may differ from the reference program's by a relative error of at most 0.0068.
Values may be sent and summed in bfloat16 or wider, within the bound.
No kernel may reach another device: no remote copies, remote signals or barrier semaphores. Data moves between devices by JAX's collectives and lax.ppermute only.
A program may use at most 192 MiB of HBM per device.

```python
import math
import jax
import jax.numpy as jnp
from jax import lax

R_DEV = 256
W = 256
F = 128
L = 1024
V = 128
P_SIZE = 256
R = 4096
SRC_BLOCK = 8
REF_BLOCK = 16


def blocked_picks(key, count, per_block):
    block_count = R // R_DEV

    def one_block(block_index):
        shuffled = jax.random.permutation(jax.random.fold_in(key, block_index), R_DEV)
        return shuffled[:per_block].astype(jnp.int32) + block_index * R_DEV
    return jax.vmap(one_block)(jnp.arange(block_count, dtype=jnp.int32)).reshape(count)


def draw_virtual_sources(key, part):
    return blocked_picks(jax.random.fold_in(key, 11), V, SRC_BLOCK)


def draw_references(key, part):
    return blocked_picks(jax.random.fold_in(key, 23), P_SIZE, REF_BLOCK)


def with_ends(values, stream_key, smallest, largest):
    index_at = [jax.random.randint(jax.random.fold_in(stream_key, axis), (), 0, length) for axis, length in enumerate(values.shape)]
    widest = values.shape.index(max(values.shape))
    beside = index_at[:widest] + [(index_at[widest] + 1) % values.shape[widest]] + index_at[widest + 1:]
    return values.at[tuple(index_at)].set(smallest).at[tuple(beside)].set(largest)


def levels(stream_key, shape, cuts, low, top_value):
    def one(axis_at, parts):
        steps = jax.random.uniform(jax.random.fold_in(jax.random.fold_in(stream_key, 6), axis_at), (parts,), jnp.float32, low / len(cuts), top_value / len(cuts))
        return jnp.repeat(jnp.exp(steps), shape[axis_at] // parts).reshape((-1,) + (1,) * (len(shape) - axis_at - 1))

    level = one(*cuts[0])
    for cut in cuts[1:]:
        level = level * one(*cut)
    return level


def normal_values(own_key, dims, deviation, limit, cuts=(), held_as=jnp.bfloat16):
    loudness = levels(own_key, dims, cuts, -0.22, 0.18) if cuts else 1.0
    values = jax.random.normal(own_key, dims, jnp.float32) * deviation * loudness
    return jnp.minimum(jnp.maximum(values, -limit), limit).astype(held_as)


def setup_inputs(seed: int = 0) -> dict:
    key_of = jax.random.split(jax.random.key(seed), 6)
    return {
        "spectra": normal_values(key_of[0], (2, W, F, R), 1.0, 6.0, ((2, 2), (3, 16))),
        "virtual_sources": draw_virtual_sources(jax.random.fold_in(key_of[5], 71), 0),
        "references": draw_references(jax.random.fold_in(key_of[5], 71), 0),
        "coda_start": with_ends(jax.random.randint(key_of[3], (V,), L // 16, L // 4), jax.random.fold_in(key_of[3], 1), L // 16, (L // 4) - 1).astype(jnp.int32),
        "coda_end": with_ends(jax.random.randint(key_of[4], (V,), 3 * L // 8, L // 2), jax.random.fold_in(key_of[4], 1), 3 * L // 8, (L // 2) - 1).astype(jnp.int32),
    }


def lag_tables(freq_count, lag_count, first_lag, lag_width):
    lag_values = first_lag + jnp.arange(lag_width, dtype=jnp.int32)
    bin_numbers = jnp.arange(freq_count, dtype=jnp.int32) + 1
    phase_steps = bin_numbers[:, None] * lag_values[None, :] % lag_count
    angles = phase_steps.astype(jnp.float32) * (2.0 * math.pi / lag_count)
    return (jnp.cos(angles), jnp.sin(angles))

def taper_weights(coda_start, coda_end, lag_count):
    lag_values = jnp.arange(lag_count, dtype=jnp.int32)
    lag_reach = jnp.where(lag_values < lag_count // 2, lag_values, lag_count - lag_values)[:, None]
    coda_first = coda_start[None, :]
    coda_last = coda_end[None, :]
    inside = (lag_reach >= coda_first) & (lag_reach < coda_last)
    window_span = (coda_last - coda_first).astype(jnp.float32)
    sine_value = jnp.sin(math.pi * ((lag_reach - coda_first).astype(jnp.float32) + 0.5) / window_span)
    return jnp.where(inside, sine_value * sine_value, jnp.zeros_like(sine_value))

def recompress(spectra_block, taper_table, lag_count):
    freq_count = spectra_block.shape[1]
    src_count = spectra_block.shape[2]
    rcv_count = spectra_block.shape[3]
    flattened = spectra_block.reshape(2 * freq_count, src_count * rcv_count)
    lag_width = min(lag_count, 256)
    accumulated = jnp.zeros((2 * freq_count, src_count * rcv_count), jnp.float32)
    for lag_block in range(lag_count // lag_width):
        first_lag = lag_block * lag_width
        cosine_table, sine_table = lag_tables(freq_count, lag_count, first_lag, lag_width)
        stacked = jnp.concatenate([cosine_table, -sine_table], axis=0)
        inverse = (stacked.T * (1.0 / math.sqrt(freq_count))).astype(jnp.bfloat16)
        forward = (stacked * (4.0 / math.sqrt(lag_count))).astype(jnp.bfloat16)
        series = jnp.dot(inverse, flattened, preferred_element_type=jnp.float32)
        weights = taper_table[first_lag:first_lag + lag_width]
        shaped = series.reshape(lag_width, src_count, rcv_count) * weights[:, :, None]
        squashed = (shaped / jnp.sqrt(1.0 + shaped * shaped)).astype(jnp.bfloat16)
        squashed = squashed.reshape(lag_width, src_count * rcv_count)
        accumulated = accumulated + jnp.dot(forward, squashed, preferred_element_type=jnp.float32)
    return accumulated.astype(jnp.bfloat16).reshape(2, freq_count, src_count, rcv_count)

def cross_spectra(sources, spectra_block, window_count):
    sources = sources.astype(jnp.float32)
    spectra_block = spectra_block.astype(jnp.float32)
    left_side = jnp.concatenate([sources[0], sources[1]], axis=0)
    right_real = jnp.concatenate([spectra_block[0], spectra_block[1]], axis=0)
    right_imag = jnp.concatenate([spectra_block[1], -spectra_block[0]], axis=0)
    real_part = jnp.einsum('wfv,wfr->fvr', left_side, right_real)
    imag_part = jnp.einsum('wfv,wfr->fvr', left_side, right_imag)
    return (jnp.stack([real_part, imag_part]) / math.sqrt(window_count)).astype(jnp.bfloat16)

def recorrelate(picked, relayed, src_total):
    picked = picked.astype(jnp.float32)
    relayed = relayed.astype(jnp.float32)
    left_side = jnp.concatenate([picked[0], picked[1]], axis=1)
    right_real = jnp.concatenate([relayed[0], relayed[1]], axis=1)
    right_imag = jnp.concatenate([relayed[1], -relayed[0]], axis=1)
    real_part = jnp.einsum('fvp,fvr->fpr', left_side, right_real)
    imag_part = jnp.einsum('fvp,fvr->fpr', left_side, right_imag)
    return jnp.stack([real_part, imag_part]) / math.sqrt(src_total)

def reference(spectra, virtual_sources, references, coda_start, coda_end):
    sources = jnp.take(spectra, virtual_sources, axis=3)
    taper_table = taper_weights(coda_start, coda_end, L)
    block_count = R // R_DEV
    blocks = spectra.reshape(2, W, F, block_count, R_DEV).transpose(3, 0, 1, 2, 4)

    def one_block(piece):
        return recompress(cross_spectra(sources, piece, W), taper_table, L)
    relayed_blocks = lax.map(one_block, blocks)
    relayed = relayed_blocks.transpose(1, 2, 3, 0, 4).reshape(2, F, V, R)
    picked = jnp.take(relayed, references, axis=3)
    result_blocks = lax.map(lambda piece: recorrelate(picked, piece, V), relayed_blocks)
    return result_blocks.transpose(1, 2, 3, 0, 4).reshape(2, F, P_SIZE, R)
```

```python
import functools
import math

import jax
import jax.numpy as jnp
from jax import lax
from jax.experimental import pallas as pl
from jax.experimental.pallas import tpu as pltpu
from jax.sharding import PartitionSpec as P


L = 1024
FIRST_LAG = L // 16
LANES = 128
QUAD = 4


NT = (((1,), (1,)), ((), ()))


def in_hbm(arrays):
    return [pltpu.with_memory_space_constraint(a, pltpu.MemorySpace.HBM) for a in arrays]


def used_lags():
    ahead = jnp.arange(FIRST_LAG, L // 2, dtype=jnp.int32)
    return jnp.concatenate([ahead, L - ahead])


def lag_tables(freq_total, freq_ids_in, freq_ids_out):
    lags = used_lags()

    def tables(freq_ids):
        steps = (freq_ids[:, None] + 1) * lags[None, :] % L
        angles = steps.astype(jnp.float32) * (2.0 * math.pi / L)
        return jnp.cos(angles), jnp.sin(angles)

    cosine, sine = tables(freq_ids_in.reshape(-1))
    shape = freq_ids_in.shape + (lags.shape[0],)
    stacked = jnp.stack([cosine.reshape(shape), -sine.reshape(shape)], axis=1)
    stacked = stacked.reshape(-1, lags.shape[0])
    inverse = (stacked.T * (1.0 / math.sqrt(freq_total))).astype(jnp.bfloat16)
    cosine, sine = tables(freq_ids_out)
    forward = jnp.concatenate([cosine, -sine], axis=0)
    forward = (forward * (4.0 / math.sqrt(L))).astype(jnp.bfloat16)
    return inverse, forward


def taper_at(first, last):
    reach = jnp.arange(FIRST_LAG, L // 2, dtype=jnp.int32)[:, None]
    first = first[..., None, :]
    last = last[..., None, :]
    inside = (reach >= first) & (reach < last)
    span = (last - first).astype(jnp.float32)
    value = jnp.sin(math.pi * ((reach - first).astype(jnp.float32) + 0.5) / span)
    return jnp.where(inside, value * value, jnp.zeros_like(value))


def select_kernel(windows, fb, x_ref, onehot_ref, xf_ref, s_ref):
    for c in range(2):
        xf_ref[:, c * windows : (c + 1) * windows, :] = jnp.swapaxes(x_ref[c], 0, 1)
    for f in range(fb):
        picked = lax.dot_general(
            onehot_ref[...], xf_ref[f], NT, preferred_element_type=jnp.float32
        )
        s_ref[f] = picked.astype(jnp.bfloat16)


def select_sources(spectra, onehot, part, parts):
    _, windows, freqs, rcvs = spectra.shape
    freqs //= parts
    count = onehot.shape[0]
    fb = min(freqs, 16)
    first = part * freqs // fb
    return pl.pallas_call(
        functools.partial(select_kernel, windows, fb),
        grid=(freqs // fb,),
        in_specs=[
            pl.BlockSpec((2, windows, fb, rcvs), lambda i: (0, 0, first + i, 0)),
            pl.BlockSpec((count, rcvs), lambda i: (0, 0)),
        ],
        out_specs=[
            pl.BlockSpec((fb, 2 * windows, rcvs), lambda i: (i, 0, 0)),
            pl.BlockSpec((fb, count, 2 * windows), lambda i: (i, 0, 0)),
        ],
        out_shape=[
            jax.ShapeDtypeStruct((freqs, 2 * windows, rcvs), spectra.dtype),
            jax.ShapeDtypeStruct((freqs, count, 2 * windows), spectra.dtype),
        ],
        compiler_params=pltpu.CompilerParams(vmem_limit_bytes=50 << 20),
        name="select",
    )(spectra, onehot)


def cross_kernel(windows, fb, steps, planes, halves, scale, *refs):
    parts, shards = len(steps), planes * QUAD
    inputs, sources = refs[:parts], refs[parts : parts + shards]
    outs, held = refs[parts + shards : -1], refs[-1]

    def multiply(x_ref):
        for f in range(fb):
            a = jnp.concatenate([s[f] for s in sources], axis=0)
            turned = jnp.concatenate([-a[:, windows:], a[:, :windows]], axis=1)
            left = jnp.concatenate([a, turned], axis=0)
            product = jnp.dot(left, x_ref[f], preferred_element_type=jnp.float32)
            product = (product * scale).astype(jnp.bfloat16)
            count = a.shape[0]
            held[0, f] = product[:count]
            held[1, f] = product[count:]

    if parts == 1:
        multiply(inputs[0])
    else:
        step = pl.program_id(0)
        first = 0
        for count, x_ref in zip(steps, inputs):
            pl.when((step >= first) & (step < first + count))(
                functools.partial(multiply, x_ref)
            )
            first += count
    total = held.shape[2] // planes
    for c in range(2):
        swapped = jnp.swapaxes(held[c], 0, 1)
        for k in range(planes):
            for h in range(halves):
                outs[k * halves + h][:, c] = swapped[
                    k * total : (k + 1) * total, :, h * LANES : (h + 1) * LANES
                ]


def cross_spectra(by_freq, planes):
    _, depth, rcvs = by_freq[0].shape
    sources = [shard for plane in planes for shard in plane]
    count = sources[0].shape[1]
    total = QUAD * count
    halves = rcvs // LANES
    fb = min(16, *[x.shape[0] for x in by_freq]) if len(by_freq) > 1 else min(16, by_freq[0].shape[0])
    steps = [x.shape[0] // fb for x in by_freq]
    freqs = sum(steps) * fb
    arrays = len(planes) * halves

    def x_spec(part):
        first = sum(steps[:part])
        return pl.BlockSpec(
            (fb, depth, rcvs), lambda i: (jnp.clip(i - first, 0, steps[part] - 1), 0, 0)
        )

    blocks = pl.pallas_call(
        functools.partial(
            cross_kernel, depth // 2, fb, steps, len(planes), halves, 1.0 / math.sqrt(depth // 2)
        ),
        grid=(sum(steps),),
        in_specs=[x_spec(part) for part in range(len(by_freq))]
        + [pl.BlockSpec((fb, count, depth), lambda i: (i, 0, 0))] * len(sources),
        out_specs=[pl.BlockSpec((total, 2, fb, LANES), lambda i: (0, 0, i, 0))] * arrays,
        out_shape=[pltpu.HBM((total, 2, freqs, LANES), jnp.bfloat16)] * arrays,
        scratch_shapes=[pltpu.VMEM((2, fb, len(planes) * total, rcvs), jnp.bfloat16)],
        compiler_params=pltpu.CompilerParams(vmem_limit_bytes=50 << 20),
        name="cross",
    )(*by_freq, *sources)
    blocks = [t.reshape(total, 2 * freqs, LANES) for t in blocks]
    return [blocks[k * halves : (k + 1) * halves] for k in range(len(planes))]


def squashed_transform(inverse_ref, forward_ref, spectrum, weights_of):
    lag_count = inverse_ref.shape[0]
    result = None
    for start in range(0, lag_count, 256):
        stop = min(start + 256, lag_count)
        series = jnp.dot(
            inverse_ref[start:stop, :], spectrum, preferred_element_type=jnp.float32
        )
        x = series * weights_of(start, stop)
        squashed = (x * lax.rsqrt(1.0 + x * x)).astype(jnp.bfloat16)
        part = jnp.dot(
            forward_ref[:, start:stop], squashed, preferred_element_type=jnp.float32
        )
        result = part if result is None else result + part
    return result.astype(jnp.bfloat16)


def rows_of(table, start, stop):
    half = table.shape[0]
    pieces = []
    while start < stop:
        at = start % half
        size = min(stop - start, half - at)
        pieces.append(table[at : at + size])
        start += size
    return pieces[0] if len(pieces) == 1 else jnp.concatenate(pieces, axis=0)


def column_of(blocks, parts, index):
    if parts == 1:
        return jnp.concatenate([b[index] for b in blocks], axis=0)
    rows = []
    for peer in range(0, len(blocks), parts):
        for c in range(2):
            for b in blocks[peer : peer + parts]:
                half = b.shape[1] // 2
                rows.append(b[index, c * half : (c + 1) * half, :])
    return jnp.concatenate(rows, axis=0)


def recompress_kernel(
    count, parts, vb, first_column, info_ref, inverse_ref, forward_ref, taper_ref, *refs
):
    blocks, out_ref, held = refs[:count], refs[count], refs[count + 1]
    step = pl.program_id(0)
    columns = taper_ref.shape[1]
    freqs = out_ref.shape[0]

    def pair(i, carry):
        v = 2 * i
        spectrum = jnp.concatenate(
            [column_of(blocks, parts, v), column_of(blocks, parts, v + 1)], axis=1
        )
        at = first_column + step * vb + v
        turned = pltpu.roll(taper_ref[...], columns - at, 1)
        lanes = (turned.shape[0], LANES)
        weights = jnp.concatenate(
            [
                jnp.broadcast_to(turned[:, 0:1], lanes),
                jnp.broadcast_to(turned[:, 1:2], lanes),
            ],
            axis=1,
        )
        result = squashed_transform(
            inverse_ref, forward_ref, spectrum, lambda a, b: rows_of(weights, a, b)
        )
        row = info_ref[step] + v
        held[row] = result[:, :LANES]
        held[row + 1] = result[:, LANES:]
        return carry

    lax.fori_loop(0, vb // 2, pair, 0, unroll=True)

    @pl.when(step == pl.num_programs(0) - 1)
    def _():
        for c in range(2):
            out_ref[:, c] = jnp.swapaxes(held[:, c * freqs : (c + 1) * freqs, :], 0, 1)


def recompress(pieces, parts, inverse, forward, taper, first_column, info):
    total, part_rows, _ = pieces[0].shape
    rows = part_rows * parts
    vb = total // QUAD
    lag_count, depth = inverse.shape
    freqs = rows // 2
    fixed = lambda i, info_ref: (0, 0)
    return pl.pallas_call(
        functools.partial(recompress_kernel, len(pieces), parts, vb, first_column),
        grid_spec=pltpu.PrefetchScalarGridSpec(
            num_scalar_prefetch=1,
            grid=(QUAD,),
            in_specs=[
                pl.BlockSpec((lag_count, depth), fixed),
                pl.BlockSpec((rows, lag_count), fixed),
                pl.BlockSpec(taper.shape, fixed),
            ]
            + [pl.BlockSpec((vb, part_rows, LANES), lambda i, info_ref: (i, 0, 0))] * len(pieces),
            out_specs=pl.BlockSpec(
                (freqs, 2, total, LANES), lambda i, info_ref: (0, 0, 0, 0)
            ),
            scratch_shapes=[pltpu.VMEM((total, rows, LANES), jnp.bfloat16)],
        ),
        out_shape=pltpu.HBM((freqs, 2, total, LANES), jnp.bfloat16),
        compiler_params=pltpu.CompilerParams(vmem_limit_bytes=50 << 20),
        name="recompress",
    )(info, inverse, forward, taper, *in_hbm(pieces))


def reference_kernel(halves, parts, per_source, lanes_ref, *refs):
    blocks, out_ref = refs[:-1], refs[-1]
    rcvs = halves * LANES
    columns = out_ref.shape[2]
    share = columns // per_source
    rows = lax.broadcasted_iota(jnp.int32, (rcvs, columns), 0)
    group = lax.broadcasted_iota(jnp.int32, (rcvs, columns), 1) // share
    hit = rows == lanes_ref[...]
    results = [None] * parts
    for j in range(per_source):
        onehot = jnp.where(hit & (group == j), 1.0, 0.0).astype(jnp.bfloat16)
        for p in range(parts):
            own = blocks[p * halves : (p + 1) * halves]
            left = jnp.concatenate([b[j] for b in own], axis=1)
            found = jnp.dot(left, onehot, preferred_element_type=jnp.float32)
            results[p] = found if j == 0 else results[p] + found
    size = results[0].shape[0] // 2
    for c in range(2):
        for p in range(parts):
            row = (c * parts + p) * size
            out_ref[0, row : row + size] = results[p][c * size : (c + 1) * size].astype(
                jnp.bfloat16
            )


def reference_columns(pieces, parts, ref_lanes, per_source):
    total, part_rows, _ = pieces[0].shape
    rows = part_rows * parts
    columns = ref_lanes.shape[1]
    halves = len(pieces) // parts
    return pl.pallas_call(
        functools.partial(reference_kernel, halves, parts, per_source),
        grid=(total // per_source,),
        in_specs=[pl.BlockSpec(ref_lanes.shape, lambda i: (0, 0))]
        + [pl.BlockSpec((per_source, part_rows, LANES), lambda i: (i, 0, 0))] * len(pieces),
        out_specs=pl.BlockSpec((1, rows, columns), lambda i: (i, 0, 0)),
        out_shape=jax.ShapeDtypeStruct((total // per_source, rows, columns), jnp.bfloat16),
        compiler_params=pltpu.CompilerParams(vmem_limit_bytes=50 << 20),
        name="refcols",
    )(ref_lanes, *in_hbm(pieces))


def reference_recompress_kernel(
    peers, per_step, per_source, info_ref, inverse_ref, forward_ref, parts_ref, *refs
):
    blocks, out_ref = refs[:peers], refs[peers]
    step = pl.program_id(0)
    columns = out_ref.shape[2]
    share = columns // per_source
    spectrum = jnp.concatenate(
        [jnp.concatenate([b[u] for b in blocks], axis=0) for u in range(per_step)], axis=1
    )
    sources = parts_ref.shape[1] // 3
    shape = (sources, per_step * columns)
    wanted = step * per_step * per_source + lax.broadcasted_iota(jnp.int32, shape, 1) // share
    pick = jnp.where(lax.broadcasted_iota(jnp.int32, shape, 0) == wanted, 1.0, 0.0)
    pick = pick.astype(jnp.bfloat16)
    weights = jnp.dot(
        parts_ref[...],
        jnp.concatenate([pick] * 3, axis=0),
        preferred_element_type=jnp.float32,
    )
    result = squashed_transform(
        inverse_ref, forward_ref, spectrum, lambda a, b: rows_of(weights, a, b)
    )
    for u in range(per_step):
        out_ref[info_ref[step * per_step + u]] = result[:, u * columns : (u + 1) * columns]


def in_parts(values):
    parts, rest = [], values
    for _ in range(3):
        part = lax.reduce_precision(rest, exponent_bits=8, mantissa_bits=7)
        parts.append(part.astype(jnp.bfloat16))
        rest = rest - part
    return jnp.concatenate(parts, axis=1)


def reference_recompress(pieces, inverse, forward, parts, devices, per_source):
    slots, rows, columns = pieces[0].shape
    lag_count, depth = inverse.shape
    peers = len(pieces)
    per_step = 2
    fixed = lambda i, info_ref: (0, 0)
    return pl.pallas_call(
        functools.partial(reference_recompress_kernel, peers, per_step, per_source),
        grid_spec=pltpu.PrefetchScalarGridSpec(
            num_scalar_prefetch=1,
            grid=(slots // per_step,),
            in_specs=[
                pl.BlockSpec((lag_count, depth), fixed),
                pl.BlockSpec((rows, lag_count), fixed),
                pl.BlockSpec(parts.shape, fixed),
            ]
            + [pl.BlockSpec((per_step, rows, columns), lambda i, info_ref: (i, 0, 0))] * peers,
            out_specs=pl.BlockSpec((slots, rows, columns), lambda i, info_ref: (0, 0, 0)),
        ),
        out_shape=jax.ShapeDtypeStruct((slots, rows, columns), jnp.bfloat16),
        compiler_params=pltpu.CompilerParams(vmem_limit_bytes=50 << 20),
        name="refpass",
    )(devices, inverse, forward, parts, *pieces)


def recorrelate_kernel(planes, halves, fb, scale, info_ref, *refs):
    relayed = refs[: planes * halves]
    picked = refs[planes * halves : -3]
    out_ref, left, right = refs[-3:]
    per_device = picked[0].shape[1]
    sources = relayed[0].shape[2]
    for k in range(planes):
        for c in range(2):
            row = pl.multiple_of(
                c * planes * sources + info_ref[k * QUAD] // QUAD * sources, sources
            )
            for f in range(fb):
                for h in range(halves):
                    right[f, pl.ds(row, sources), h * LANES : (h + 1) * LANES] = relayed[
                        h * planes + k
                    ][f, c]
    for slot in range(planes * QUAD):
        row = pl.multiple_of(info_ref[slot] * per_device, per_device)
        for f in range(fb):
            left[f, pl.ds(row, per_device), :] = picked[slot][f].astype(left.dtype)
    for f in range(fb):
        p = left[f].astype(jnp.bfloat16)
        half = p.shape[1] // 2
        turned = jnp.concatenate([-p[:, half:], p[:, :half]], axis=1)
        r = right[f]
        out_ref[0, f] = jnp.dot(p, r, preferred_element_type=jnp.float32) * scale
        out_ref[1, f] = jnp.dot(turned, r, preferred_element_type=jnp.float32) * scale


def recorrelate(relayed, picked, devices):
    halves, planes = len(relayed), len(relayed[0])
    relayed = [r for half in relayed for r in half]
    freqs, _, sources, _ = relayed[0].shape
    per_device, depth = picked[0].shape[1:]
    fb = min(freqs, 8)
    refs_total = per_device * len(picked)
    rcvs = halves * LANES
    left_type = jnp.bfloat16 if per_device % 16 == 0 else jnp.float32
    return pl.pallas_call(
        functools.partial(
            recorrelate_kernel, planes, halves, fb, 1.0 / math.sqrt(planes * sources)
        ),
        grid_spec=pltpu.PrefetchScalarGridSpec(
            num_scalar_prefetch=1,
            grid=(freqs // fb,),
            in_specs=[
                pl.BlockSpec((fb, 2, sources, LANES), lambda i, info_ref: (i, 0, 0, 0))
            ]
            * len(relayed)
            + [pl.BlockSpec((fb, per_device, depth), lambda i, info_ref: (i, 0, 0))]
            * len(picked),
            out_specs=pl.BlockSpec(
                (2, fb, refs_total, rcvs), lambda i, info_ref: (0, i, 0, 0)
            ),
            scratch_shapes=[
                pltpu.VMEM((fb, refs_total, depth), left_type),
                pltpu.VMEM((fb, 2 * planes * sources, rcvs), jnp.bfloat16),
            ],
        ),
        out_shape=jax.ShapeDtypeStruct((2, freqs, refs_total, rcvs), jnp.float32),
        compiler_params=pltpu.CompilerParams(vmem_limit_bytes=58 << 20),
        name="recorrelate",
    )(devices, *in_hbm(relayed), *in_hbm(picked))


def moved(value, planes, source_of):
    pairs = [(source_of(z, q), z * QUAD + q) for z in range(planes) for q in range(QUAD)]
    return lax.ppermute(value, "rcv", pairs)


def own_plane(x, planes):
    across = moved(x, planes, lambda z, q: z * QUAD + (q ^ 2))
    beside = moved(x, planes, lambda z, q: z * QUAD + (q ^ 1))
    both = moved(across, planes, lambda z, q: z * QUAD + (q ^ 1))
    return [x, beside, across, both]


def further_planes(x, planes):
    return [
        own_plane(moved(x, planes, lambda z, q: (z + k) % planes * QUAD + q), planes)
        for k in range(1, planes)
    ]


def plane_groups(planes):
    groups = [(0,), (1,), tuple(range(2, planes))]
    return [g for g in groups if g and g[0] < planes]


def body(spectra, virtual_sources, references, coda_start, coda_end):
    _, _, freqs, rcvs = spectra.shape
    rcv_index = lax.axis_index("rcv")
    rcv_total = lax.axis_size("rcv")
    frq_index = lax.axis_index("frq")
    frq_total = lax.axis_size("frq")
    planes = rcv_total // QUAD
    halves = rcvs // LANES
    first_rcv = rcv_index * rcvs
    local_rows = jnp.arange(rcvs, dtype=jnp.int32)
    per_device = virtual_sources.shape[0] // rcv_total
    ref_share = references.shape[0] // rcv_total
    own_picks = (
        lax.dynamic_slice_in_dim(virtual_sources, rcv_index * per_device, per_device) - first_rcv
    )
    onehot = (own_picks[:, None] == local_rows[None, :]).astype(jnp.bfloat16)
    parts = part_count(freqs)
    by_freq, selected = [], []
    for part in range(parts):
        found = select_sources(spectra, onehot, part, parts)
        by_freq.append(found[0])
        selected.append(found[1])

    place = jnp.arange(QUAD, dtype=jnp.int32) ^ (rcv_index % QUAD)
    plane_of = (rcv_index // QUAD + jnp.arange(planes, dtype=jnp.int32)) % planes
    devices = (plane_of[:, None] * QUAD + place[None, :]).reshape(-1)
    slot_start = coda_start.reshape(rcv_total, per_device)[devices]
    slot_end = coda_end.reshape(rcv_total, per_device)[devices]
    taper = taper_at(slot_start.reshape(-1), slot_end.reshape(-1))
    own_freqs = jnp.arange(freqs, dtype=jnp.int32)
    peers = (frq_index + jnp.arange(frq_total, dtype=jnp.int32)) % frq_total
    inverse, forward = lag_tables(
        freqs * frq_total,
        peers[:, None] * freqs + own_freqs[None, :],
        frq_index * freqs + own_freqs,
    )
    own_refs = (
        lax.dynamic_slice_in_dim(references, rcv_index * ref_share, ref_share) - first_rcv
    )
    ref_lanes = jnp.tile(own_refs, per_device)[None]

    def exchanged(value):
        pieces = [value]
        for s in range(1, frq_total):
            pairs = [((y + s) % frq_total, y) for y in range(frq_total)]
            pieces.append(lax.ppermute(value, "frq", pairs))
        return pieces

    info = place * per_device
    near = []
    for part in range(parts):
        shards = own_plane(selected[part], planes)
        near.append(cross_spectra([by_freq[part]], [shards])[0])
    whole = selected[0] if parts == 1 else jnp.concatenate(selected, axis=0)
    sources = further_planes(whole, planes)
    cross = []
    for group in plane_groups(planes)[1:]:
        cross += cross_spectra(by_freq, [sources[k - 1] for k in group])

    ref_cross = []
    for k in range(planes):
        pieces = [t for blocks in near for t in blocks] if k == 0 else cross[k - 1]
        ref_cross.append(
            reference_columns(pieces, 1 if k else parts, ref_lanes, per_device)
        )
    ref_pieces = exchanged(jnp.concatenate(ref_cross, axis=0))
    ref_relayed = reference_recompress(
        ref_pieces, inverse, forward, in_parts(taper), devices, per_device
    )
    own_picked = (
        ref_relayed.reshape(rcv_total, 2, freqs, per_device, ref_share)
        .transpose(2, 4, 1, 0, 3)
        .reshape(freqs, ref_share, 2 * rcv_total * per_device)
    )
    picked = own_plane(own_picked, planes)
    for plane in further_planes(own_picked, planes):
        picked += plane

    relayed = []
    for h in range(halves):
        row = []
        for k in range(planes):
            if k == 0:
                each = [exchanged(near[p][h]) for p in range(parts)]
                pieces = [piece for peer in zip(*each) for piece in peer]
            else:
                pieces = exchanged(cross[k - 1][h])
            row.append(
                recompress(
                    pieces,
                    1 if k else parts,
                    inverse,
                    forward,
                    taper,
                    k * QUAD * per_device,
                    info,
                )
            )
        relayed.append(row)
    return recorrelate(relayed, picked, devices)


def part_count(freqs):
    return 2 if freqs % 32 == 0 else 1


def solution(mesh):
    return jax.shard_map(
        body,
        mesh=mesh,
        in_specs=(P(None, None, "frq", "rcv"), P(), P(), P(), P()),
        out_specs=P(None, "frq", None, "rcv"),
        check_vma=False,
    )
```
